32 devices in a mesh: dp: 8 (over z, x), enc: 4 (over y, core).
Axes of the slice: x: 2, y: 2, z: 4, core: 2. Of those that a mesh axis runs over, the one named last changes fastest.
Arguments:
- chars: int32 [393216, 50], P('dp'), may hold values from 0 to 261
- char_table: bfloat16 [262, 16], replicated, may hold values from -6 to 6
- conv_weight: bfloat16 [7, 16, 2048], P(None, None, 'enc'), may hold values from -0.75 to 0.75
- conv_bias: float32 [2048], P('enc'), may hold values from -3 to 3
- hw_weight: bfloat16 [2, 2048, 2, 2048], P(None, None, None, 'enc'), may hold values from -0.125 to 0.125
- hw_bias: float32 [2, 2, 2048], P(None, None, 'enc'), may hold values from -4 to 4
- proj_weight: bfloat16 [2048, 512], P('enc'), may hold values from -0.125 to 0.125
- proj_bias: float32 [512], P('enc'), may hold values from -3 to 3
- owner_types: int32 [8192], P('dp'), may hold values from 0 to 49151, as said below
- requests: int32 [8, 8, 512], P('dp'), may hold values from -1 to 1023, as said below
- tok_slot: int32 [65536], P('dp'), may hold values from 0 to 4095, as said below
- d_tokens: bfloat16 [65536, 512], P('dp', 'enc'), may hold values from -0.59765625 to 0.59765625
Outputs:
- token_vectors: bfloat16 [65536, 512], P('dp', 'enc')
- d_features: bfloat16 [8192, 2048], P('dp', 'enc')
- d_highway: float32 [2, 2048, 2, 2048], P(None, 'dp', None, 'enc')
- d_projection: float32 [2048, 512], P('enc', 'dp')
The draws below stay inside these ranges and needn't reach their ends.
Inputs may be any that keep to these rules, and one draw needn't show every extreme that they name: `owner_types`: entries o * 1024 to (o + 1) * 1024 - 1 are distinct rows of owner o's 49152 rows of chars; every owner's list holds its first and its last row. `requests`: list (r, o) holds 128 to 512 distinct positions of owner o's unique list, then -1 entries. Every position of every owner's list is asked for by some replica. In every draw one owner receives full lists (512 positions) from every replica, and some list is not full. `tok_slot`: token t of replica r names a slot o * 512 + k with requests[r, o, k] >= 0; every such slot is named by at least one token of replica r.
All inputs are finite; a program needn't handle non-finite values.
Results may differ from the reference program's by a relative error of at most 0.015.
Values may be sent and summed in bfloat16 or wider, within the bound.
No kernel may reach another device: no remote copies, remote signals or barrier semaphores. Data moves between devices by JAX's collectives and lax.ppermute only.
A program may use at most 192 MiB of HBM per device.

```python
import math
import jax
import jax.numpy as jnp
from jax import lax

F = 2048
P_SIZE = 512
CE = 16
CH = 50
NCHAR = 262
TAPS = 7
HW_LAYERS = 2
TYPES_DEV = 49152
UNIQ = 1024
CAP = 512
TOK_REP = 8192
TYPES = 393216
TOKENS = 65536
N_DP = 8
N_ENC = 4


def request_plan(key):
    base = jax.random.fold_in(key, 4242)
    keys = jax.random.split(base, 8)
    owners = 4 * UNIQ // CAP
    quarter = CAP // 4
    level = jax.random.randint(keys[0], (owners,), 1, 5)
    cutback = jax.random.randint(keys[1], (owners, owners), 0, CAP // 8 + 1)
    counts = jnp.maximum(level[None, :] * quarter - cutback, quarter)
    full_owner = jax.random.randint(keys[2], (), 0, owners)
    lucky = jax.random.randint(keys[3], (), 0, owners)
    columns = jnp.arange(owners)
    replicas = jnp.arange(owners)
    counts = jnp.where(columns[None, :] == full_owner, CAP, counts)
    light = (replicas[:, None] == (lucky + 1) % owners) & (columns[None, :] == (full_owner + 1) % owners)
    counts = jnp.where(light, quarter, counts)
    heavy = (replicas[:, None] == lucky) & (columns[None, :] == owners - 1)
    counts = jnp.where(heavy, CAP, counts)
    list_keys = jax.random.split(keys[4], owners * owners)
    shuffles = jax.vmap(lambda one_key: jax.random.permutation(one_key, UNIQ))(list_keys)
    shuffles = shuffles.reshape(owners, owners, UNIQ).astype(jnp.int32)
    position = jnp.arange(UNIQ, dtype=jnp.int32)
    others = (position[None, None, :] % owners != replicas[:, None, None]).astype(jnp.int32)
    scores = others * 2 ** 22 + shuffles
    picks = jnp.argsort(scores, axis=2, stable=True)[:, :, :CAP].astype(jnp.int32)
    live = jnp.arange(CAP)[None, None, :] < counts[:, :, None]
    requests = jnp.where(live, picks, -1).astype(jnp.int32)
    slots = owners * CAP
    live_flat = live.reshape(owners, slots).astype(jnp.int32)
    slot_keys = jax.random.split(keys[5], owners)
    slot_shuffle = jax.vmap(lambda one_key: jax.random.permutation(one_key, slots))(slot_keys).astype(jnp.int32)
    order = jnp.argsort((1 - live_flat) * 2 ** 22 + slot_shuffle, axis=1, stable=True).astype(jnp.int32)
    live_total = jnp.sum(live_flat, axis=1)
    draws = jax.random.randint(keys[6], (owners, TOK_REP), 0, 2 ** 20) % live_total[:, None]
    token_index = jnp.arange(TOK_REP, dtype=jnp.int32)[None, :]
    chosen = jnp.where(token_index < live_total[:, None], token_index, draws * draws // live_total[:, None])
    token_slots = jnp.take_along_axis(order, chosen, axis=1)
    token_keys = jax.random.split(keys[7], owners)
    token_shuffle = jax.vmap(lambda one_key: jax.random.permutation(one_key, TOK_REP))(token_keys).astype(jnp.int32)
    token_slots = jnp.take_along_axis(token_slots, token_shuffle, axis=1)
    return (requests, token_slots.reshape(-1).astype(jnp.int32))


def draw_requests(key, part):
    return request_plan(key)[0]


def draw_tok_slot(key, part):
    return request_plan(key)[1]


def owner_list(one_key):
    first_key, second_key = jax.random.split(one_key)
    inner = jax.random.permutation(first_key, TYPES_DEV - 2)[:UNIQ - 2].astype(jnp.int32) + 1
    ends = jnp.array([0, TYPES_DEV - 1], dtype=jnp.int32)
    listed = jnp.concatenate([ends, inner])
    order = jax.random.permutation(second_key, UNIQ)
    return listed[order]


def draw_owner_types(key, part):
    owners = 4 * UNIQ // CAP
    type_keys = jax.random.split(jax.random.fold_in(key, 77), owners)
    chosen = jax.vmap(owner_list)(type_keys)
    return chosen.reshape(-1).astype(jnp.int32)


def set_ends(values, own_key, smallest, high):
    dims = values.shape
    index_at = [jax.random.randint(jax.random.fold_in(own_key, axis), (), 0, dims[axis]) for axis in range(len(dims))]
    values = values.at[tuple(index_at)].set(smallest)
    longest = dims.index(max(dims))
    index_at[longest] = (index_at[longest] + 1) % dims[longest]
    return values.at[tuple(index_at)].set(high)


def steps_of(key, extent, cuts, least, high):
    level, own = 1.0, jax.random.fold_in(key, 6)
    for dim, shards_of in cuts:
        heights = jnp.exp(jax.random.uniform(jax.random.fold_in(own, dim), (shards_of,), jnp.float32, least / len(cuts), high / len(cuts)))
        level = level * jnp.repeat(heights, extent[dim] // shards_of).reshape([-1 if axis == dim else 1 for axis in range(len(extent))])
    return level


def gaussian(rng, extent, spread, limit, cuts=(), held_as=jnp.bfloat16):
    entries = spread * jax.random.normal(rng, extent, jnp.float32)
    if cuts:
        entries = entries * steps_of(rng, extent, cuts, -0.22, 0.18)
    return jnp.clip(entries, -limit, limit).astype(held_as)


def setup_inputs(seed: int = 0) -> dict:
    key_of = jax.random.split(jax.random.key(seed), 13)
    return {
        "chars": set_ends(jax.random.randint(key_of[0], (TYPES, CH), 0, NCHAR), jax.random.fold_in(key_of[0], 1), 0, NCHAR - 1).astype(jnp.int32),
        "char_table": gaussian(key_of[1], (NCHAR, CE), 1.0, 6.0),
        "conv_weight": gaussian(key_of[2], (TAPS, CE, F), (4 * CE) ** -0.5, 0.75, ((2, 4),)),
        "conv_bias": gaussian(key_of[3], (F,), 0.5, 3.0, ((0, 4),), jnp.float32),
        "hw_weight": gaussian(key_of[4], (HW_LAYERS, F, 2, F), F ** -0.5, 0.125, ((3, 4),)),
        "hw_bias": gaussian(key_of[5], (HW_LAYERS, 2, F), 1.0, 4.0, ((2, 4),), jnp.float32),
        "proj_weight": gaussian(key_of[6], (F, P_SIZE), F ** -0.5, 0.125, ((0, 4),)),
        "proj_bias": gaussian(key_of[7], (P_SIZE,), 0.5, 3.0, ((0, 4),), jnp.float32),
        "owner_types": draw_owner_types(jax.random.fold_in(key_of[12], 71), 0),
        "requests": draw_requests(jax.random.fold_in(key_of[12], 71), 0),
        "tok_slot": draw_tok_slot(jax.random.fold_in(key_of[12], 71), 0),
        "d_tokens": gaussian(key_of[11], (TOKENS, P_SIZE), 0.1, 0.59765625, ((0, 8), (1, 4))),
    }


def filter_widths(total_filters):
    filter_index = jnp.arange(total_filters, dtype=jnp.int32)
    width = jnp.ones((total_filters,), jnp.int32)
    for share in (1, 2, 4, 8, 16, 32):
        width = width + (filter_index >= share * total_filters // 64).astype(jnp.int32)
    return width


def encode_words(word_chars, char_table, conv_weight, conv_bias):
    taps, embed_width, total_filters = conv_weight.shape
    length = word_chars.shape[1]
    width = filter_widths(total_filters)
    tap_mask = jnp.arange(taps, dtype=jnp.int32)[:, None] < width[None, :]
    kernel = jnp.where(tap_mask[:, None, :], conv_weight, jnp.zeros_like(conv_weight))
    kernel = kernel.reshape(taps * embed_width, total_filters).astype(jnp.float32)
    valid = jnp.arange(length, dtype=jnp.int32)[:, None] + width[None, :] <= length

    def encode_block(block_chars):
        vectors = char_table[block_chars]
        shifted = jnp.pad(vectors, ((0, 0), (0, taps - 1), (0, 0)))
        windows = jnp.concatenate([shifted[:, tap:tap + length, :] for tap in range(taps)], axis=2)
        conv = jnp.einsum('bpk,kf->bpf', windows.astype(jnp.float32), kernel)
        conv = jnp.where(valid[None], conv, -jnp.inf)
        return jnp.maximum(jnp.max(conv, axis=1) + conv_bias, 0.0).astype(jnp.bfloat16)

    rows = word_chars.shape[0]
    block = math.gcd(rows, 128)
    pooled = lax.map(encode_block, word_chars.reshape(rows // block, block, length))
    return pooled.reshape(rows, total_filters)


def reference(chars, char_table, conv_weight, conv_bias, hw_weight, hw_bias, proj_weight, proj_bias, owner_types, requests, tok_slot, d_tokens):
    layers = hw_weight.shape[0]
    total_filters = hw_weight.shape[1]
    owners = N_DP
    owner_base = (jnp.arange(owners, dtype=jnp.int32) * TYPES_DEV)[:, None]
    global_types = (owner_types.reshape(owners, UNIQ) + owner_base).reshape(-1)
    word_chars = chars[global_types]
    features = encode_words(word_chars, char_table, conv_weight, conv_bias)
    rows = features.shape[0]

    layer_input = features
    saved = []
    for layer in range(layers):
        weight_rows = hw_weight[layer].reshape(total_filters, 2 * total_filters)
        pre = jnp.dot(layer_input, weight_rows, preferred_element_type=jnp.float32)
        transform = pre[:, :total_filters] + hw_bias[layer, 0]
        gate = jax.nn.sigmoid(pre[:, total_filters:] + hw_bias[layer, 1])
        saved.append((layer_input, transform, gate))
        mixed = gate * jax.nn.silu(transform) + (1.0 - gate) * layer_input.astype(jnp.float32)
        layer_input = mixed.astype(jnp.bfloat16)
    top = layer_input
    encoded = (jnp.dot(top, proj_weight, preferred_element_type=jnp.float32) + proj_bias).astype(jnp.bfloat16)

    slots = owners * CAP
    owner_rows = jnp.arange(owners, dtype=jnp.int32)[None, :, None] * UNIQ
    slot_rows = (owner_rows + jnp.maximum(requests, 0)).reshape(owners, slots)
    token_slots = tok_slot.reshape(owners, TOK_REP)
    token_rows = jnp.take_along_axis(slot_rows, token_slots, axis=1).reshape(-1)
    token_vectors = encoded[token_rows]

    segment_index = (jnp.arange(owners, dtype=jnp.int32)[:, None] * slots + token_slots).reshape(-1)
    slot_grads = jax.ops.segment_sum(d_tokens.astype(jnp.float32), segment_index, num_segments=owners * slots)
    slot_grads = slot_grads.astype(jnp.bfloat16)
    targets = jnp.where(requests >= 0, owner_rows + requests, rows).reshape(-1)
    row_grads = jax.ops.segment_sum(slot_grads.astype(jnp.float32), targets, num_segments=rows + 1)[:rows]
    row_grads = row_grads.astype(jnp.bfloat16)

    d_projection = jnp.dot(top.T, row_grads, preferred_element_type=jnp.float32)
    upstream = jnp.dot(row_grads, proj_weight.T, preferred_element_type=jnp.float32)
    group = total_filters // N_ENC
    grads = [None] * layers
    for layer in reversed(range(layers)):
        layer_in, transform, gate = saved[layer]
        weight = hw_weight[layer]
        sigma = jax.nn.sigmoid(transform)
        activated = transform * sigma
        slope = sigma * (1.0 + transform * (1.0 - sigma))
        transform_grad = upstream * gate * slope
        gate_grad = upstream * (activated - layer_in.astype(jnp.float32)) * gate * (1.0 - gate)
        pre_grads = jnp.stack([transform_grad, gate_grad], axis=1).astype(jnp.bfloat16)
        whole_grads = jnp.dot(layer_in.T, pre_grads.reshape(rows, 2 * total_filters), preferred_element_type=jnp.float32)
        grads[layer] = whole_grads.reshape(total_filters, 2, total_filters)
        back = upstream * (1.0 - gate)
        for part in range(N_ENC):
            grads_part = pre_grads[:, :, part * group:(part + 1) * group].reshape(rows, 2 * group)
            weight_part = weight[:, :, part * group:(part + 1) * group].reshape(total_filters, 2 * group)
            term = lax.dot_general(grads_part, weight_part, (((1,), (1,)), ((), ())), preferred_element_type=jnp.float32)
            back = back + lax.optimization_barrier(term.astype(jnp.bfloat16)).astype(jnp.float32)
        upstream = back
    d_features = upstream.astype(jnp.bfloat16)
    return token_vectors, d_features, jnp.stack(grads), d_projection
```

```python
import functools
import jax
import jax.numpy as jnp
from jax import lax
from jax.experimental import pallas as pl
from jax.experimental.pallas import tpu as pltpu
from jax.sharding import PartitionSpec as P

CHUNKS = 8
HIGH = 4

def pick_kernel(bits, types_ref, charsT_ref, out_ref, chars_v, packed_v, sems):
    length, total = charsT_ref.shape
    uniq = types_ref.shape[0]
    fold = packed_v.shape[0]
    step = total // CHUNKS
    copies = []
    for c in range(CHUNKS):
        cp = pltpu.make_async_copy(charsT_ref.at[:, c * step:(c + 1) * step], chars_v.at[:, c * step:(c + 1) * step], sems.at[c])
        cp.start()
        copies.append(cp)
    width = 512
    for c in range(CHUNKS):
        copies[c].wait()
        def pack(k, _):
            cols = pl.ds(pl.multiple_of(c * step + k * width, width), width)
            word = chars_v[0:fold, cols]
            row, shift = fold, bits
            while row < length:
                take = min(fold, length - row)
                part = chars_v[row:row + take, cols] << shift
                if take < fold:
                    part = jnp.concatenate([part, jnp.zeros((fold - take, width), jnp.int32)], axis=0)
                word = word | part
                row += take
                shift += bits
            packed_v[:, cols] = word
            return 0
        lax.fori_loop(0, step // width, pack, 0)
    lane = lax.broadcasted_iota(jnp.int32, (fold, 128), 1)
    for g in range(uniq // 128):
        def body(i, acc):
            for k in range(16):
                w = i * 16 + k
                t = types_ref[g * 128 + w]
                col = pl.multiple_of((t // 128) * 128, 128)
                acc = jnp.where(lane == w, pltpu.roll(packed_v[:, pl.ds(col, 128)], (w - t) & 127, axis=1), acc)
            return acc
        out_ref[g] = lax.fori_loop(0, 8, body, jnp.zeros((fold, 128), jnp.int32))

def conv_kernel(taps, length, bits, ids_ref, table_ref, wk_ref, bias_ref, width_ref, out_ref, ids_v, vec_v, acc_v):
    groups128, fold, _ = ids_ref.shape
    uniq = groups128 * 128
    shifts, filters, depth = wk_ref.shape
    embed = table_ref.shape[0]
    mask = (1 << bits) - 1
    for g in range(groups128):
        word = ids_ref[g]
        for k in range(-(-length // fold)):
            take = min(fold, length - k * fold)
            ids_v[g, k * fold:k * fold + take, :] = ((word >> (k * bits)) & mask)[:take]
    vec_v[length * embed:, :] = jnp.zeros((vec_v.shape[0] - length * embed, uniq), vec_v.dtype)
    n_tab = table_ref.shape[1] // 128
    tabs = [table_ref[:, k * 128:(k + 1) * 128] for k in range(n_tab)]
    def embed_body(p, _):
        for g in range(groups128):
            idx = jnp.broadcast_to(ids_v[g, pl.ds(p, 1), :], (embed, 128))
            low = idx & 127
            res = jnp.take_along_axis(tabs[0], low, axis=1)
            for k in range(1, n_tab):
                res = jnp.where(idx >= 128 * k, jnp.take_along_axis(tabs[k], low, axis=1), res)
            vec_v[pl.ds(pl.multiple_of(p * embed, embed), embed), g * 128:(g + 1) * 128] = res.astype(vec_v.dtype)
        return 0
    lax.fori_loop(0, length, embed_body, 0)
    groups = -(-length // shifts)
    nt = 256
    def nbody(n, _):
        cols = pl.ds(pl.multiple_of(n * nt, nt), nt)
        best = None
        for g in range(groups):
            rhs = vec_v[g * shifts * embed: g * shifts * embed + depth, cols]
            for s in range(shifts):
                p = g * shifts + s
                if p >= length:
                    break
                r = jnp.dot(wk_ref[s], rhs, preferred_element_type=jnp.float32)
                if p + taps > length:
                    r = jnp.where(width_ref[...] + p <= length, r, -jnp.inf)
                best = r if best is None else jnp.maximum(best, r)
            if g < groups - 1:
                acc_v[...] = best if g == 0 else jnp.maximum(best, acc_v[...])
                best = None
        best = jnp.maximum(best, acc_v[...])
        out_ref[:, cols] = jnp.maximum(best + bias_ref[...], 0.0).astype(out_ref.dtype)
        return 0
    lax.fori_loop(0, uniq // nt, nbody, 0)

def pick_words(chars, owner_types, alphabet):
    total, length = chars.shape
    uniq = owner_types.shape[0]
    bits = (alphabet - 1).bit_length()
    per = 31 // bits
    fold = -(-(-(-length // per)) // 8) * 8
    return pl.pallas_call(
        functools.partial(pick_kernel, bits),
        out_shape=jax.ShapeDtypeStruct((uniq // 128, fold, 128), jnp.int32),
        in_specs=[pl.BlockSpec(memory_space=pltpu.SMEM), pl.BlockSpec(memory_space=pl.ANY)],
        out_specs=pl.BlockSpec(memory_space=pltpu.VMEM),
        scratch_shapes=[pltpu.VMEM((length, total), jnp.int32), pltpu.VMEM((fold, total), jnp.int32), pltpu.SemaphoreType.DMA((CHUNKS,))],
        compiler_params=pltpu.CompilerParams(vmem_limit_bytes=56 << 20),
        cost_estimate=pl.CostEstimate(flops=0, bytes_accessed=30 << 20, transcendentals=0),
        name="pick_words",
    )(owner_types, chars.T)

def conv_operands(char_table, conv_weight, conv_bias, width):
    taps, embed, filters = conv_weight.shape
    alphabet = char_table.shape[0]
    depth = 256
    shifts = depth // embed - taps + 1
    nalpha = -(-alphabet // 128) * 128
    tap_mask = jnp.arange(taps, dtype=jnp.int32)[:, None] < width[None, :]
    kernel = jnp.where(tap_mask[:, None, :], conv_weight, jnp.zeros_like(conv_weight))
    kT = kernel.reshape(taps * embed, filters).T
    wk = jnp.stack([jnp.pad(kT, ((0, 0), (s * embed, depth - (s + taps) * embed))) for s in range(shifts)])
    tabT = jnp.pad(char_table.T.astype(jnp.float32), ((0, 0), (0, nalpha - alphabet)))
    return tabT, wk, conv_bias[:, None], width[:, None]

def encode(ids, operands, taps, length, alphabet):
    tabT, wk, bias, width = operands
    shifts, filters, depth = wk.shape
    embed = tabT.shape[0]
    uniq = ids.shape[0] * 128
    bits = (alphabet - 1).bit_length()
    groups = -(-length // shifts)
    vrows = ((groups - 1) * shifts) * embed + depth
    return pl.pallas_call(
        functools.partial(conv_kernel, taps, length, bits),
        out_shape=jax.ShapeDtypeStruct((filters, uniq), jnp.bfloat16),
        in_specs=[pl.BlockSpec(memory_space=pltpu.VMEM)] * 5,
        out_specs=pl.BlockSpec(memory_space=pltpu.VMEM),
        scratch_shapes=[pltpu.VMEM((ids.shape[0], -(-length // 8) * 8, 128), jnp.int32), pltpu.VMEM((vrows, uniq), jnp.bfloat16), pltpu.VMEM((filters, 256), jnp.float32)],
        compiler_params=pltpu.CompilerParams(vmem_limit_bytes=40 << 20),
        cost_estimate=pl.CostEstimate(flops=2 * uniq * length * 256 * filters, bytes_accessed=4 << 20, transcendentals=0),
        name="word_encoder",
    )(ids, tabT, wk, bias, width)

def spread(row, lanes):
    return jnp.broadcast_to(row, (lanes, row.shape[1])).T

def sum_kernel(low, index_ref, data_ref, out_ref, acc_ref):
    step = pl.program_id(0)
    index = index_ref[0]
    block, cols = data_ref.shape
    low_index = index & (low - 1)
    high_index = index >> (low.bit_length() - 1)
    hot = (lax.broadcasted_iota(jnp.int32, (low, block), 0) == low_index).astype(jnp.bfloat16)
    high = spread(high_index, cols)
    data = data_ref[...]
    zero = jnp.zeros_like(data)
    wide = jnp.concatenate([jnp.where(high == h, data, zero) for h in range(HIGH)], axis=1)
    part = jnp.dot(hot, wide, preferred_element_type=jnp.float32)
    @pl.when(step == 0)
    def _():
        acc_ref[...] = part
    @pl.when(step > 0)
    def _():
        acc_ref[...] += part
    @pl.when(step == pl.num_programs(0) - 1)
    def _():
        for h in range(HIGH):
            out_ref[h * low:(h + 1) * low, :] = acc_ref[:, h * cols:(h + 1) * cols].astype(out_ref.dtype)

def sum_rows(data, index, segments, block):
    count, cols = data.shape
    low = segments // HIGH
    return pl.pallas_call(
        functools.partial(sum_kernel, low),
        grid=(count // block,),
        out_shape=jax.ShapeDtypeStruct((segments, cols), data.dtype),
        in_specs=[pl.BlockSpec((1, 1, block), lambda i: (i, 0, 0)), pl.BlockSpec((block, cols), lambda i: (i, 0))],
        out_specs=pl.BlockSpec((segments, cols), lambda i: (0, 0)),
        scratch_shapes=[pltpu.VMEM((low, HIGH * cols), jnp.float32)],
        compiler_params=pltpu.CompilerParams(vmem_limit_bytes=40 << 20),
        cost_estimate=pl.CostEstimate(flops=4 * count * segments * cols, bytes_accessed=2 * cols * (count + segments), transcendentals=0),
        name="sum_rows",
    )(index.reshape(count // block, 1, block), data)

def take_kernel(low, high_count, index_ref, table_ref, out_ref, wide_ref):
    cols = table_ref.shape[1]
    @pl.when(pl.program_id(0) == 0)
    def _():
        for h in range(high_count):
            wide_ref[:, h * cols:(h + 1) * cols] = table_ref[h * low:(h + 1) * low, :]
    index = index_ref[0]
    block = index.shape[1]
    low_index = spread(index & (low - 1), 128)
    lane = lax.broadcasted_iota(jnp.int32, (block, 128), 1)
    hot = jnp.concatenate([(lane + 128 * k == low_index).astype(jnp.bfloat16) for k in range(low // 128)], axis=1)
    got = jnp.dot(hot, wide_ref[...], preferred_element_type=jnp.float32)
    high = spread(index >> (low.bit_length() - 1), cols)
    out = got[:, :cols]
    for h in range(1, high_count):
        out = jnp.where(high == h, got[:, h * cols:(h + 1) * cols], out)
    out_ref[...] = out.astype(out_ref.dtype)

def take_rows(table, index, block, high):
    count = index.shape[0]
    rows, cols = table.shape
    low = rows // high
    return pl.pallas_call(
        functools.partial(take_kernel, low, high),
        grid=(count // block,),
        out_shape=jax.ShapeDtypeStruct((count, cols), table.dtype),
        in_specs=[pl.BlockSpec((1, 1, block), lambda i: (i, 0, 0)), pl.BlockSpec((rows, cols), lambda i: (0, 0))],
        out_specs=pl.BlockSpec((block, cols), lambda i: (i, 0)),
        scratch_shapes=[pltpu.VMEM((low, high * cols), table.dtype)],
        compiler_params=pltpu.CompilerParams(vmem_limit_bytes=40 << 20),
        cost_estimate=pl.CostEstimate(flops=2 * count * rows * cols, bytes_accessed=2 * cols * (count + rows), transcendentals=0),
        name="take_rows",
    )(index.reshape(count // block, 1, block), table)


PARTS = 2
F32, BF16 = jnp.float32, jnp.bfloat16


def filter_widths(filter_index, total_filters):
    width = jnp.ones(filter_index.shape, jnp.int32)
    for share in (1, 2, 4, 8, 16, 32):
        width = width + (filter_index >= share * total_filters // 64).astype(jnp.int32)
    return width


def dot(a, b, contract):
    return lax.dot_general(a, b, ((contract[:1], contract[1:]), ((), ())), preferred_element_type=F32)


def swap(x, axis, flip):
    size = lax.axis_size(axis)
    return lax.ppermute(x, axis, [(i, i ^ flip) for i in range(size)])


def gather_enc(x):
    blocks = [x] + [None] * (lax.axis_size("enc") - 1)
    for j in range(2, len(blocks), 2):
        blocks[j] = swap(x, "enc", j)
    for j in range(1, len(blocks), 2):
        blocks[j] = swap(blocks[j - 1], "enc", 1)
    return blocks


def scatter_enc(term):
    size = lax.axis_size("enc")
    others = []
    for j in list(range(2, size, 2)) + [0]:
        passed = swap(term(j + 1).astype(BF16), "enc", 1)
        here = term(j) + passed.astype(F32)
        if j:
            others.append(swap(here.astype(BF16), "enc", j))
    for other in others:
        here = here + other.astype(F32)
    return here


def scatter_dp(halves, order):
    keep, send = halves
    for step, bit in enumerate(order):
        got = swap(send, "dp", 1 << bit)
        if step == len(order) - 1:
            return keep.astype(F32) + got.astype(F32)
        half = keep.shape[0] // 2
        send = (keep[half:].astype(F32) + got[half:].astype(F32)).astype(BF16)
        keep = (keep[:half].astype(F32) + got[:half].astype(F32)).astype(BF16)


def relative_rows(blocks, order):
    size, groups = lax.axis_size("enc"), lax.axis_size("dp")
    e, d = lax.axis_index("enc"), lax.axis_index("dp")
    per_block = blocks.shape[0] // size
    per_group = blocks.shape[0] // groups
    pieces = []
    for k in range(groups):
        flip = 0
        for place, bit in enumerate(order):
            if k >> (len(order) - 1 - place) & 1:
                flip |= 1 << bit
        first = (d ^ flip) * per_group
        owner = first // per_block
        start = (owner ^ e) * per_block + first - owner * per_block
        pieces.append(lax.dynamic_slice_in_dim(blocks, start, per_group, axis=0))
    return jnp.concatenate(pieces, axis=0)


def per_device(
    chars,
    char_table,
    conv_weight,
    conv_bias,
    hw_weight,
    hw_bias,
    proj_weight,
    proj_bias,
    owner_types,
    requests,
    tok_slot,
    d_tokens,
):
    taps, embed_width, local = conv_weight.shape
    layers, total_filters = hw_weight.shape[:2]
    length, alphabet = chars.shape[1], char_table.shape[0]
    rows = owner_types.shape[0]
    enc_size, dp_size = lax.axis_size("enc"), lax.axis_size("dp")
    e = lax.axis_index("enc")
    width = filter_widths(e * local + jnp.arange(local, dtype=jnp.int32), total_filters)
    bits = dp_size.bit_length() - 1
    middle = bits // 2
    order_a = list(range(bits))
    order_b = [middle] + [b for b in range(bits) if b != middle]

    ids = pick_words(chars, owner_types, alphabet)
    operands = conv_operands(char_table, conv_weight, conv_bias, width)
    per_part = ids.shape[0] // PARTS
    parts = range(PARTS)
    part_rows = rows // PARTS
    layer_in = [
        encode(ids[k * per_part : (k + 1) * per_part], operands, taps, length, alphabet) for k in parts
    ]

    slot_total = requests.shape[1] * requests.shape[2]
    asked = lax.all_to_all(requests[0], "dp", split_axis=0, concat_axis=0, tiled=True).reshape(-1)
    slot_grads = sum_rows(d_tokens, tok_slot, slot_total, min(1024, tok_slot.shape[0]))
    arrived = lax.all_to_all(
        slot_grads.reshape(requests.shape[1], requests.shape[2], -1), "dp", split_axis=0, concat_axis=0, tiled=True
    ).reshape(slot_total, -1)
    row_grads = sum_rows(arrived, asked, rows, min(1024, slot_total))
    full_grads = jnp.concatenate(gather_enc(row_grads), axis=1)
    proj_cols = proj_weight.shape[1] // enc_size
    proj = jnp.concatenate(
        [lax.dynamic_slice_in_dim(proj_weight, (e ^ j) * proj_cols, proj_cols, axis=1) for j in range(enc_size)], axis=1
    )

    weights = []
    for layer in range(layers):
        weights.append(
            jnp.concatenate(
                [lax.dynamic_slice_in_dim(hw_weight[layer], (e ^ j) * local, local, axis=0) for j in range(enc_size)],
                axis=0,
            ).reshape(total_filters, 2 * local)
        )
    bias = hw_bias[..., None]

    saved = []
    half = total_filters // 2
    for layer in range(layers):
        wholes, transforms, gates, nexts = [], [], [], []
        for k in parts:
            blocks = gather_enc(layer_in[k])
            near = jnp.concatenate(blocks[: enc_size // 2], axis=0)
            far = jnp.concatenate(blocks[enc_size // 2 :], axis=0)
            pre = dot(weights[layer][:half], near, (0, 0)) + dot(weights[layer][half:], far, (0, 0))
            transform = pre[:local] + bias[layer, 0]
            gate = jax.nn.sigmoid(pre[local:] + bias[layer, 1])
            mixed = gate * jax.nn.silu(transform) + (1.0 - gate) * layer_in[k].astype(F32)
            wholes.append(jnp.concatenate([near, far], axis=0))
            transforms.append(transform)
            gates.append(gate)
            nexts.append(mixed.astype(BF16))
        saved.append((layer_in, jnp.concatenate(wholes, axis=1), transforms, gates))
        layer_in = nexts
    top = layer_in

    encoded = []
    for k in parts:
        encoded.append(
            scatter_enc(lambda j: dot(top[k], proj[:, j * proj_cols : (j + 1) * proj_cols], (0, 0)))
        )
    encoded = (jnp.concatenate(encoded, axis=0) + proj_bias).astype(BF16)
    outgoing = take_rows(encoded, jnp.maximum(asked, 0), min(1024, slot_total), 2)
    returned = lax.all_to_all(
        outgoing.reshape(dp_size, slot_total // dp_size, -1), "dp", split_axis=0, concat_axis=0, tiled=True
    ).reshape(slot_total, -1)
    token_vectors = take_rows(returned, tok_slot, min(1024, tok_slot.shape[0]), HIGH)

    top_all = jnp.concatenate(top, axis=1)
    d_proj = dot(full_grads, top_all, (0, 1)).astype(BF16)
    d_proj = relative_rows(d_proj, order_a)
    d_proj_half = d_proj.shape[0] // 2
    d_projection = scatter_dp((d_proj[:d_proj_half], d_proj[d_proj_half:]), order_a).T

    upstream = [
        dot(proj, full_grads[k * part_rows : (k + 1) * part_rows], (1, 1)) for k in parts
    ]
    grads = [None] * layers
    for layer in reversed(range(layers)):
        layer_ins, whole, transforms, gates = saved[layer]
        pres = []
        for k in parts:
            transform, gate = transforms[k], gates[k]
            sigma = jax.nn.sigmoid(transform)
            activated = transform * sigma
            slope = sigma * (1.0 + transform * (1.0 - sigma))
            transform_grad = upstream[k] * gate * slope
            gate_grad = upstream[k] * (activated - layer_ins[k].astype(F32)) * gate * (1.0 - gate)
            pre_grads = jnp.concatenate([transform_grad, gate_grad], axis=0).astype(BF16)
            pres.append(pre_grads)
            summed = scatter_enc(
                lambda j: dot(weights[layer][j * local : (j + 1) * local], pre_grads, (1, 0)).astype(BF16).astype(F32)
            )
            upstream[k] = upstream[k] * (1.0 - gate) + summed
        pre_all = jnp.concatenate(pres, axis=1)
        pair = []
        for g, order in enumerate((order_a, order_b)):
            ordered = relative_rows(whole, order)
            side = pre_all[g * local : (g + 1) * local]
            sent = dot(ordered[half:], side, (1, 1)).astype(BF16)
            kept = dot(ordered[:half], side, (1, 1)).astype(BF16)
            pair.append(scatter_dp((kept, sent), order))
        grads[layer] = jnp.stack(pair, axis=1)
    d_features = jnp.concatenate(upstream, axis=1).astype(BF16).T
    return (token_vectors, d_features, jnp.stack(grads), d_projection)


def solution(mesh):
    return jax.shard_map(
        per_device,
        mesh=mesh,
        in_specs=(
            P("dp", None),
            P(),
            P(None, None, "enc"),
            P("enc"),
            P(None, None, None, "enc"),
            P(None, None, "enc"),
            P("enc", None),
            P("enc"),
            P("dp"),
            P("dp", None, None),
            P("dp"),
            P("dp", "enc"),
        ),
        out_specs=(P("dp", "enc"), P("dp", "enc"), P(None, "dp", None, "enc"), P("enc", "dp")),
        check_vma=False,
    )
```

```python
import functools
import jax
import jax.numpy as jnp
from jax import lax
from jax.experimental import pallas as pl
from jax.experimental.pallas import tpu as pltpu
from jax.sharding import PartitionSpec as P


CHUNKS = 8
HIGH = 4


def pick_kernel(bits, types_ref, charsT_ref, out_ref, chars_v, packed_v, sems):
    length, total = charsT_ref.shape
    uniq = types_ref.shape[0]
    fold = packed_v.shape[0]
    step = total // CHUNKS
    copies = []
    for c in range(CHUNKS):
        cp = pltpu.make_async_copy(charsT_ref.at[:, c * step:(c + 1) * step], chars_v.at[:, c * step:(c + 1) * step], sems.at[c])
        cp.start()
        copies.append(cp)
    width = 512
    for c in range(CHUNKS):
        copies[c].wait()
        def pack(k, _):
            cols = pl.ds(pl.multiple_of(c * step + k * width, width), width)
            word = chars_v[0:fold, cols]
            row, shift = fold, bits
            while row < length:
                take = min(fold, length - row)
                part = chars_v[row:row + take, cols] << shift
                if take < fold:
                    part = jnp.concatenate([part, jnp.zeros((fold - take, width), jnp.int32)], axis=0)
                word = word | part
                row += take
                shift += bits
            packed_v[:, cols] = word
            return 0
        lax.fori_loop(0, step // width, pack, 0)
    lane = lax.broadcasted_iota(jnp.int32, (fold, 128), 1)
    for g in range(uniq // 128):
        def body(i, acc):
            for k in range(16):
                w = i * 16 + k
                t = types_ref[g * 128 + w]
                col = pl.multiple_of((t // 128) * 128, 128)
                acc = jnp.where(lane == w, pltpu.roll(packed_v[:, pl.ds(col, 128)], (w - t) & 127, axis=1), acc)
            return acc
        out_ref[g] = lax.fori_loop(0, 8, body, jnp.zeros((fold, 128), jnp.int32))


def conv_kernel(taps, length, bits, ids_ref, table_ref, wk_ref, bias_ref, width_ref, out_ref, ids_v, vec_v, acc_v):
    groups128, fold, _ = ids_ref.shape
    uniq = groups128 * 128
    shifts, _, depth = wk_ref.shape
    embed = table_ref.shape[0]
    mask = (1 << bits) - 1
    for g in range(groups128):
        word = ids_ref[g]
        for k in range(-(-length // fold)):
            take = min(fold, length - k * fold)
            ids_v[g, k * fold:k * fold + take, :] = ((word >> (k * bits)) & mask)[:take]
    vec_v[length * embed:, :] = jnp.zeros((vec_v.shape[0] - length * embed, uniq), vec_v.dtype)
    n_tab = table_ref.shape[1] // 128
    tabs = [table_ref[:, k * 128:(k + 1) * 128] for k in range(n_tab)]
    def embed_body(p, _):
        for g in range(groups128):
            idx = jnp.broadcast_to(ids_v[g, pl.ds(p, 1), :], (embed, 128))
            low = idx & 127
            res = jnp.take_along_axis(tabs[0], low, axis=1)
            for k in range(1, n_tab):
                res = jnp.where(idx >= 128 * k, jnp.take_along_axis(tabs[k], low, axis=1), res)
            vec_v[pl.ds(pl.multiple_of(p * embed, embed), embed), g * 128:(g + 1) * 128] = res.astype(vec_v.dtype)
        return 0
    lax.fori_loop(0, length, embed_body, 0)
    groups = -(-length // shifts)
    nt = 256
    def nbody(n, _):
        cols = pl.ds(pl.multiple_of(n * nt, nt), nt)
        best = None
        for g in range(groups):
            rhs = vec_v[g * shifts * embed: g * shifts * embed + depth, cols]
            for s in range(shifts):
                p = g * shifts + s
                if p >= length:
                    break
                r = jnp.dot(wk_ref[s], rhs, preferred_element_type=jnp.float32)
                if p + taps > length:
                    r = jnp.where(width_ref[...] + p <= length, r, -jnp.inf)
                best = r if best is None else jnp.maximum(best, r)
            if g < groups - 1:
                acc_v[...] = best if g == 0 else jnp.maximum(best, acc_v[...])
                best = None
        best = jnp.maximum(best, acc_v[...])
        out_ref[:, cols] = jnp.maximum(best + bias_ref[...], 0.0).astype(out_ref.dtype)
        return 0
    lax.fori_loop(0, uniq // nt, nbody, 0)


def pick_words(chars, owner_types, alphabet):
    total, length = chars.shape
    uniq = owner_types.shape[0]
    bits = (alphabet - 1).bit_length()
    per = 31 // bits
    fold = -(-(-(-length // per)) // 8) * 8
    return pl.pallas_call(
        functools.partial(pick_kernel, bits),
        out_shape=jax.ShapeDtypeStruct((uniq // 128, fold, 128), jnp.int32),
        in_specs=[pl.BlockSpec(memory_space=pltpu.SMEM), pl.BlockSpec(memory_space=pl.ANY)],
        out_specs=pl.BlockSpec(memory_space=pltpu.VMEM),
        scratch_shapes=[pltpu.VMEM((length, total), jnp.int32), pltpu.VMEM((fold, total), jnp.int32), pltpu.SemaphoreType.DMA((CHUNKS,))],
        compiler_params=pltpu.CompilerParams(vmem_limit_bytes=60 << 20),
        cost_estimate=pl.CostEstimate(flops=0, bytes_accessed=30 << 20, transcendentals=0),
        name="pick_words",
    )(owner_types, chars.T)


def conv_operands(char_table, conv_weight, conv_bias, width):
    taps, embed, filters = conv_weight.shape
    alphabet = char_table.shape[0]
    depth = 256
    shifts = depth // embed - taps + 1
    nalpha = -(-alphabet // 128) * 128
    tap_mask = jnp.arange(taps, dtype=jnp.int32)[:, None] < width[None, :]
    kernel = jnp.where(tap_mask[:, None, :], conv_weight, jnp.zeros_like(conv_weight))
    kT = kernel.reshape(taps * embed, filters).T
    wk = jnp.stack([jnp.pad(kT, ((0, 0), (s * embed, depth - (s + taps) * embed))) for s in range(shifts)])
    tabT = jnp.pad(char_table.T.astype(jnp.float32), ((0, 0), (0, nalpha - alphabet)))
    return tabT, wk, conv_bias[:, None], width[:, None]


def encode(ids, operands, taps, length, alphabet):
    tabT, wk, bias, width = operands
    shifts, filters, depth = wk.shape
    embed = tabT.shape[0]
    uniq = ids.shape[0] * 128
    bits = (alphabet - 1).bit_length()
    groups = -(-length // shifts)
    vrows = ((groups - 1) * shifts) * embed + depth
    return pl.pallas_call(
        functools.partial(conv_kernel, taps, length, bits),
        out_shape=jax.ShapeDtypeStruct((filters, uniq), jnp.bfloat16),
        in_specs=[pl.BlockSpec(memory_space=pltpu.VMEM)] * 5,
        out_specs=pl.BlockSpec(memory_space=pltpu.VMEM),
        scratch_shapes=[pltpu.VMEM((ids.shape[0], -(-length // 8) * 8, 128), jnp.int32), pltpu.VMEM((vrows, uniq), jnp.bfloat16), pltpu.VMEM((filters, 256), jnp.float32)],
        compiler_params=pltpu.CompilerParams(vmem_limit_bytes=60 << 20),
        cost_estimate=pl.CostEstimate(flops=2 * uniq * length * 256 * filters, bytes_accessed=4 << 20, transcendentals=0),
        name="word_encoder",
    )(ids, tabT, wk, bias, width)


def spread(row, lanes):
    return jnp.broadcast_to(row, (lanes, row.shape[1])).T


def sum_kernel(low, index_ref, data_ref, out_ref, acc_ref):
    step = pl.program_id(0)
    index = index_ref[0]
    block, cols = data_ref.shape
    low_index = index & (low - 1)
    high_index = index >> (low.bit_length() - 1)
    hot = (lax.broadcasted_iota(jnp.int32, (low, block), 0) == low_index).astype(jnp.bfloat16)
    high = spread(high_index, cols)
    data = data_ref[...]
    zero = jnp.zeros_like(data)
    wide = jnp.concatenate([jnp.where(high == h, data, zero) for h in range(HIGH)], axis=1)
    part = jnp.dot(hot, wide, preferred_element_type=jnp.float32)
    @pl.when(step == 0)
    def _():
        acc_ref[...] = part
    @pl.when(step > 0)
    def _():
        acc_ref[...] += part
    @pl.when(step == pl.num_programs(0) - 1)
    def _():
        for h in range(HIGH):
            out_ref[h * low:(h + 1) * low, :] = acc_ref[:, h * cols:(h + 1) * cols].astype(out_ref.dtype)


def sum_rows(data, index, segments, block):
    count, cols = data.shape
    low = segments // HIGH
    return pl.pallas_call(
        functools.partial(sum_kernel, low),
        grid=(count // block,),
        out_shape=jax.ShapeDtypeStruct((segments, cols), data.dtype),
        in_specs=[pl.BlockSpec((1, 1, block), lambda i: (i, 0, 0)), pl.BlockSpec((block, cols), lambda i: (i, 0))],
        out_specs=pl.BlockSpec((segments, cols), lambda i: (0, 0)),
        scratch_shapes=[pltpu.VMEM((low, HIGH * cols), jnp.float32)],
        compiler_params=pltpu.CompilerParams(vmem_limit_bytes=60 << 20),
        cost_estimate=pl.CostEstimate(flops=4 * count * segments * cols, bytes_accessed=2 * cols * (count + segments), transcendentals=0),
        name="sum_rows",
    )(index.reshape(count // block, 1, block), data)


def take_kernel(low, high_count, index_ref, table_ref, out_ref, wide_ref):
    cols = table_ref.shape[1]
    @pl.when(pl.program_id(0) == 0)
    def _():
        for h in range(high_count):
            wide_ref[:, h * cols:(h + 1) * cols] = table_ref[h * low:(h + 1) * low, :]
    index = index_ref[0]
    block = index.shape[1]
    low_index = spread(index & (low - 1), 128)
    lane = lax.broadcasted_iota(jnp.int32, (block, 128), 1)
    hot = jnp.concatenate([(lane + 128 * k == low_index).astype(jnp.bfloat16) for k in range(low // 128)], axis=1)
    got = jnp.dot(hot, wide_ref[...], preferred_element_type=jnp.float32)
    high = spread(index >> (low.bit_length() - 1), cols)
    out = got[:, :cols]
    for h in range(1, high_count):
        out = jnp.where(high == h, got[:, h * cols:(h + 1) * cols], out)
    out_ref[...] = out.astype(out_ref.dtype)


def take_rows(table, index, block, high):
    count = index.shape[0]
    rows, cols = table.shape
    low = rows // high
    return pl.pallas_call(
        functools.partial(take_kernel, low, high),
        grid=(count // block,),
        out_shape=jax.ShapeDtypeStruct((count, cols), table.dtype),
        in_specs=[pl.BlockSpec((1, 1, block), lambda i: (i, 0, 0)), pl.BlockSpec((rows, cols), lambda i: (0, 0))],
        out_specs=pl.BlockSpec((block, cols), lambda i: (i, 0)),
        scratch_shapes=[pltpu.VMEM((low, high * cols), table.dtype)],
        compiler_params=pltpu.CompilerParams(vmem_limit_bytes=60 << 20),
        cost_estimate=pl.CostEstimate(flops=2 * count * rows * cols, bytes_accessed=2 * cols * (count + rows), transcendentals=0),
        name="take_rows",
    )(index.reshape(count // block, 1, block), table)


def split_kernel(tiles, kinds, e_ref, w_ref, out_ref):
    size = 256
    groups = tiles * kinds
    each = size // groups
    row = lax.broadcasted_iota(jnp.int32, (size, size), 0)
    col = lax.broadcasted_iota(jnp.int32, (size, size), 1)
    kind, tile, inner = row // (tiles * each), row // each % tiles, row % each
    order = (col == inner * groups + tile * kinds + kind).astype(jnp.bfloat16)
    for b in range(w_ref.shape[1] // size):
        got = jnp.dot(order, w_ref[0, b * size:(b + 1) * size, :], preferred_element_type=jnp.float32).astype(out_ref.dtype)
        for g in range(groups):
            out_ref[0, b * each:(b + 1) * each, g * 128:(g + 1) * 128] = got[g * each:(g + 1) * each, :]


def split_weights(hw, e, layer):
    layers, total, kinds, local = hw.shape
    tiles = local // 128
    block = min(local, 512)
    per = local // block
    flat = hw.reshape(layers, total, kinds, tiles, 128).transpose(0, 1, 3, 2, 4).reshape(layers, total * tiles * kinds, 128)
    return pl.pallas_call(
        functools.partial(split_kernel, tiles, kinds),
        grid_spec=pltpu.PrefetchScalarGridSpec(
            num_scalar_prefetch=1,
            grid=(total // block,),
            in_specs=[pl.BlockSpec((1, block * tiles * kinds, 128), lambda i, e: (layer, ((i // per) ^ e[0]) * per + i % per, 0))],
            out_specs=pl.BlockSpec((1, block, kinds * local), lambda i, e: (0, i, 0)),
        ),
        out_shape=jax.ShapeDtypeStruct((1, total, kinds * local), hw.dtype),
        compiler_params=pltpu.CompilerParams(vmem_limit_bytes=60 << 20),
        cost_estimate=pl.CostEstimate(flops=total * tiles * kinds * 256 * 256, bytes_accessed=4 * total * kinds * local, transcendentals=0),
        name="split_weights",
    )(e.reshape(1), flat)[0]


def layer_kernel(count, place_ref, *refs):
    blocks, (weight_ref, bias_ref), (whole_a_ref, whole_b_ref, transform_ref, gate_ref, mixed_ref), (turned_ref, whole_ref) = (
        refs[:count], refs[count:count + 2], refs[count + 2:count + 7], refs[count + 7:])
    local = blocks[0].shape[0]
    chunks = place_ref.shape[0] // 2
    each = local * count // chunks
    @pl.when(pl.program_id(0) == 0)
    def _():
        for j in range(count):
            turned_ref[:, j * local:(j + 1) * local] = weight_ref[j * local:(j + 1) * local, :].T
    for c in range(chunks):
        part = blocks[c * each // local][c * each % local:c * each % local + each, :]
        whole_ref[c * each:(c + 1) * each, :] = part
        whole_a_ref[pl.ds(pl.multiple_of(place_ref[c] * each, each), each), :] = part
        whole_b_ref[pl.ds(pl.multiple_of(place_ref[chunks + c] * each, each), each), :] = part
    pre = jnp.dot(turned_ref[...], whole_ref[...], preferred_element_type=jnp.float32)
    transform = pre[:local] + bias_ref[0]
    gate = jax.nn.sigmoid(pre[local:] + bias_ref[1])
    transform_ref[...] = transform
    gate_ref[...] = gate
    mixed = gate * (transform * jax.nn.sigmoid(transform)) + (1.0 - gate) * blocks[0][...].astype(jnp.float32)
    mixed_ref[...] = mixed.astype(mixed_ref.dtype)


def highway_layer(blocks, weight, bias, places):
    local, rows = blocks[0].shape
    total, wide = weight.shape
    tile = min(rows, 256)
    side = lambda height: pl.BlockSpec((height, tile), lambda i: (0, i))
    return pl.pallas_call(
        functools.partial(layer_kernel, len(blocks)),
        grid=(rows // tile,),
        out_shape=(
            jax.ShapeDtypeStruct((total, rows), jnp.bfloat16),
            jax.ShapeDtypeStruct((total, rows), jnp.bfloat16),
            jax.ShapeDtypeStruct((local, rows), jnp.float32),
            jax.ShapeDtypeStruct((local, rows), jnp.float32),
            jax.ShapeDtypeStruct((local, rows), jnp.bfloat16),
        ),
        in_specs=[pl.BlockSpec(memory_space=pltpu.SMEM)] + [side(local)] * len(blocks) + [
            pl.BlockSpec((total, wide), lambda i: (0, 0)),
            pl.BlockSpec((2, local, 1), lambda i: (0, 0, 0)),
        ],
        out_specs=(side(total), side(total), side(local), side(local), side(local)),
        scratch_shapes=[pltpu.VMEM((wide, total), jnp.bfloat16), pltpu.VMEM((total, tile), jnp.bfloat16)],
        compiler_params=pltpu.CompilerParams(vmem_limit_bytes=60 << 20),
        cost_estimate=pl.CostEstimate(flops=2 * rows * total * wide, bytes_accessed=2 * total * wide + 14 * local * rows + 6 * total * rows, transcendentals=2 * local * rows),
        name="highway_layer",
    )(places, *blocks, weight, bias)


F32, BF16 = jnp.float32, jnp.bfloat16


def filter_widths(filter_index, total_filters):
    width = jnp.ones(filter_index.shape, jnp.int32)
    for share in (1, 2, 4, 8, 16, 32):
        width = width + (filter_index >= share * total_filters // 64).astype(jnp.int32)
    return width


def dot(a, b, contract):
    return lax.dot_general(a, b, ((contract[:1], contract[1:]), ((), ())), preferred_element_type=F32)


def after(x, *others):
    return lax.optimization_barrier((x, others))[0]


def swap(x, axis, flip):
    size = lax.axis_size(axis)
    return lax.ppermute(x, axis, [(i, i ^ flip) for i in range(size)])


def gather_far(x):
    return [x] + [swap(x, "enc", j) for j in range(2, lax.axis_size("enc"), 2)]


def gather_near(blocks, *cover):
    blocks = [blocks[0]] + [after(b, cover) for b in blocks[1:]]
    return [b for block in blocks for b in (block, swap(block, "enc", 1))]


def scatter_far(term):
    size = lax.axis_size("enc")
    others = []
    for j in list(range(2, size, 2)) + [0]:
        passed = swap(term(j + 1).astype(BF16), "enc", 1)
        here = term(j) + passed.astype(F32)
        if j:
            others.append(swap(here.astype(BF16), "enc", j))
    return here, others


def scatter_near(parts, *cover):
    here, others = parts
    for other in others:
        here = here + after(other, cover).astype(F32)
    return here


def send_dp(pair, order, step):
    return swap(pair[1], "dp", 1 << order[step])


def merge_dp(pair, got, last=False):
    keep = pair[0]
    if last:
        return keep.astype(F32) + got.astype(F32)
    half = keep.shape[0] // 2
    kept, sent = ((keep[k : k + half].astype(F32) + got[k : k + half].astype(F32)).astype(BF16) for k in (0, half))
    return kept, sent


def group_places(orders):
    groups, size = lax.axis_size("dp"), lax.axis_size("enc")
    chunk = jnp.arange(groups, dtype=jnp.int32)
    per = groups // size
    flip = ((lax.axis_index("enc") ^ (chunk // per)) * per + chunk % per) ^ lax.axis_index("dp")
    return jnp.concatenate(
        [sum(((flip >> bit) & 1) << (len(order) - 1 - place) for place, bit in enumerate(order)) for order in orders]
    ).astype(jnp.int32)


def ask_step(held, bit):
    mine = (lax.axis_index("dp") >> bit) & 1
    held = held.reshape(held.shape[0], 2, held.shape[1] // 2, held.shape[2])
    got = swap(lax.dynamic_index_in_dim(held, 1 - mine, 1, keepdims=False), "dp", 1 << bit)
    return lax.dynamic_index_in_dim(held, mine, 1, keepdims=False), got


def ask_merge(kept, got, bit):
    mine = (lax.axis_index("dp") >> bit) & 1
    held = jnp.where(mine == 0, jnp.stack([kept, got], axis=1), jnp.stack([got, kept], axis=1))
    return held.reshape(-1, held.shape[2], held.shape[3])


def relative_rows(blocks, order):
    size, groups = lax.axis_size("enc"), lax.axis_size("dp")
    e, d = lax.axis_index("enc"), lax.axis_index("dp")
    per_block = blocks.shape[0] // size
    per_group = blocks.shape[0] // groups
    pieces = []
    for k in range(groups):
        flip = 0
        for place, bit in enumerate(order):
            if k >> (len(order) - 1 - place) & 1:
                flip |= 1 << bit
        first = (d ^ flip) * per_group
        owner = first // per_block
        start = (owner ^ e) * per_block + first - owner * per_block
        pieces.append(lax.dynamic_slice_in_dim(blocks, start, per_group, axis=0))
    return jnp.concatenate(pieces, axis=0)


def per_device(
    chars,
    char_table,
    conv_weight,
    conv_bias,
    hw_weight,
    hw_bias,
    proj_weight,
    proj_bias,
    owner_types,
    requests,
    tok_slot,
    d_tokens,
):
    taps, _, local = conv_weight.shape
    _, total_filters = hw_weight.shape[:2]
    length, alphabet = chars.shape[1], char_table.shape[0]
    rows = owner_types.shape[0]
    enc_size, dp_size = lax.axis_size("enc"), lax.axis_size("dp")
    e = lax.axis_index("enc")
    width = filter_widths(e * local + jnp.arange(local, dtype=jnp.int32), total_filters)
    bits = dp_size.bit_length() - 1
    middle = bits // 2
    order_a = list(range(bits))
    order_b = [middle] + [b for b in range(bits) if b != middle]

    kept, got = ask_step(requests, bits - 1)
    ids = pick_words(chars, owner_types, alphabet)
    operands = conv_operands(char_table, conv_weight, conv_bias, width)
    asked = ask_merge(kept, after(got, ids), bits - 1)
    kept, got = ask_step(asked, bits - 2)
    features = encode(ids, operands, taps, length, alphabet)
    half = total_filters // 2
    bias = hw_bias[..., None]
    slot_total = requests.shape[1] * requests.shape[2]
    proj_cols = proj_weight.shape[1] // enc_size
    proj = jnp.concatenate(
        [lax.dynamic_slice_in_dim(proj_weight, (e ^ j) * proj_cols, proj_cols, axis=1) for j in range(enc_size)], axis=1
    )

    def slopes(layer_in, transform, gate, upstream):
        sigma = jax.nn.sigmoid(transform)
        activated = transform * sigma
        slope = sigma * (1.0 + transform * (1.0 - sigma))
        transform_grad = upstream * gate * slope
        gate_grad = upstream * (activated - layer_in.astype(F32)) * gate * (1.0 - gate)
        return jnp.concatenate([transform_grad, gate_grad], axis=0).astype(BF16)

    def back(weight, pre_grads):
        return lambda j: dot(weight[j * local : (j + 1) * local], pre_grads, (1, 0)).astype(BF16).astype(F32)

    def weight_grads(ordered, pre_grads):
        pair = []
        for g, order in enumerate((order_a, order_b)):
            side = pre_grads[g * local : (g + 1) * local]
            sent = dot(ordered[g][half:], side, (1, 1)).astype(BF16)
            kept = dot(ordered[g][:half], side, (1, 1)).astype(BF16)
            pair.append((kept, sent))
        return pair

    orders = (order_a, order_b)
    places = group_places(orders)

    def start(pairs, step):
        return [send_dp(pair, order, step) for pair, order in zip(pairs, orders)]

    def merge(pairs, gots, last=False):
        return [merge_dp(pair, got, last) for pair, got in zip(pairs, gots)]

    far_0 = gather_far(features)
    weight_0 = split_weights(after(hw_weight, features), e, 0)
    asked = ask_merge(kept, after(got, features), bits - 2)
    for bit in reversed(range(bits - 2)):
        kept, got = ask_step(asked, bit)
        asked = ask_merge(kept, got, bit)
    asked = asked.reshape(-1)
    slot_grads = sum_rows(d_tokens, after(tok_slot, weight_0), slot_total, min(1024, tok_slot.shape[0]))
    arrived = lax.all_to_all(
        slot_grads.reshape(requests.shape[1], requests.shape[2], -1), "dp", split_axis=0, concat_axis=0, tiled=True
    ).reshape(slot_total, -1)
    blocks_0 = gather_near(far_0, slot_grads)
    *ordered_0, transform_0, gate_0, input_1 = highway_layer(blocks_0, weight_0, bias[0], places)

    far_1 = gather_far(input_1)
    weight_1 = split_weights(after(hw_weight, input_1), e, 1)
    row_grads = sum_rows(after(arrived, weight_1), asked, rows, min(1024, slot_total))
    far_rows = gather_far(row_grads)
    blocks_1 = gather_near(far_1, row_grads)
    full_grads = jnp.concatenate(gather_near(far_rows), axis=1)
    *ordered_1, transform_1, gate_1, top = highway_layer(blocks_1, weight_1, bias[1], places)
    upstream_2 = dot(proj, full_grads, (1, 1))

    terms = [dot(top, proj[:, j * proj_cols : (j + 1) * proj_cols], (0, 0)) for j in range(enc_size)]
    parts_enc = scatter_far(lambda j: terms[j])
    pre_1 = slopes(input_1, after(transform_1, terms), gate_1, upstream_2)
    parts_1 = scatter_far(back(weight_1, pre_1))
    d_proj = dot(full_grads, after(top, parts_1[0]), (0, 1)).astype(BF16)
    d_proj = relative_rows(d_proj, order_a)
    pair_1 = weight_grads(ordered_1, after(pre_1, d_proj))
    groups = dp_size // 2
    d_proj = d_proj.reshape(2, groups, -1, local)
    pair_1[0] = [
        jnp.concatenate([x.reshape(groups, -1, local), d_proj[k]], axis=1).reshape(-1, local)
        for k, x in enumerate(pair_1[0])
    ]
    got_1 = start(pair_1, 0)
    encoded = (scatter_near(parts_enc, pair_1) + proj_bias).astype(BF16)
    outgoing = take_rows(encoded, jnp.maximum(asked, 0), min(1024, slot_total), 2)
    returned = lax.all_to_all(
        outgoing.reshape(dp_size, slot_total // dp_size, -1), "dp", split_axis=0, concat_axis=0, tiled=True
    ).reshape(slot_total, -1)

    upstream_1 = upstream_2 * (1.0 - gate_1) + scatter_near(parts_1, outgoing)
    pre_0 = slopes(features, transform_0, gate_0, upstream_1)
    pair_0 = weight_grads(ordered_0, pre_0)
    got_0 = start(pair_0, 0)
    for step in range(1, bits):
        pair_1 = merge(pair_1, after(got_1, pair_0))
        got_1 = start(pair_1, step)
    parts_0 = scatter_far(back(weight_0, after(pre_0, pair_0)))
    pair_0 = merge(pair_0, got_0)
    got_0 = start(pair_0, 1)
    grads_1 = merge(pair_1, after(got_1, pair_0), last=True)
    d_projection = grads_1[0][total_filters // dp_size :].T
    grads_1[0] = grads_1[0][: total_filters // dp_size]
    upstream_0 = upstream_1 * (1.0 - gate_0) + scatter_near(parts_0, pair_0)
    token_vectors = take_rows(returned, after(tok_slot, pair_0), min(1024, tok_slot.shape[0]), HIGH)
    for step in range(2, bits):
        pair_0 = merge(pair_0, got_0)
        got_0 = start(pair_0, step)
    grads_0 = merge(pair_0, got_0, last=True)
    grads = [jnp.stack(grads_0, axis=1), jnp.stack(grads_1, axis=1)]
    d_features = upstream_0.astype(BF16).T
    return (token_vectors, d_features, jnp.stack(grads), d_projection)


def solution(mesh):
    return shard(mesh)


def shard(mesh):
    return jax.shard_map(
        per_device,
        mesh=mesh,
        in_specs=(
            P("dp", None),
            P(),
            P(None, None, "enc"),
            P("enc"),
            P(None, None, None, "enc"),
            P(None, None, "enc"),
            P("enc", None),
            P("enc"),
            P("dp"),
            P("dp", None, None),
            P("dp"),
            P("dp", "enc"),
        ),
        out_specs=(P("dp", "enc"), P("dp", "enc"), P(None, "dp", None, "enc"), P("enc", "dp")),
        check_vma=False,
    )
```
